32 devices in a mesh: grp: 2 (over y), seg: 16 (over z, x, core).
Axes of the slice: x: 2, y: 2, z: 4, core: 2. Of those that a mesh axis runs over, the one named last changes fastest.
Arguments:
- strain: bfloat16 [524288], P(('grp', 'seg')), parts along dimension 0, may hold values from -6 to 6
- templates: bfloat16 [128, 512], P('seg'), may hold values from -6 to 6
Outputs:
- profile: float32 [32, 128], P(('grp', 'seg')), parts along dimension 0
- overall: float32 [256], P('grp'), parts along dimension 0
The draws below stay inside these ranges and needn't reach their ends.
There are 2 independent parts, one for each index of `grp`. The reference program is written for one: setup_inputs(seed, part) draws one part's arguments, and reference() takes and returns one part's arrays. A program takes and returns all parts, laid end to end along the dimension named above; an argument that names none is the same for every part. Nothing has to cross between parts.
All inputs are finite; a program needn't handle non-finite values.
Results may differ from the reference program's by a relative error of at most 0.0003.
Values may be sent and summed in bfloat16 or wider, within the bound.
A program may use at most 256 MiB of HBM per device.

```python
import jax
import jax.numpy as jnp
from jax import lax

QUERIES = 128
M = 512
SEG_LEN = 16384
SAMPLES = 262144
N_SEG = 16


def block_levels(rng, extent, cuts, low, high):
    def one(position, shards_of):
        draws = jax.random.uniform(jax.random.fold_in(jax.random.fold_in(rng, 6), position), (shards_of,), jnp.float32, low / len(cuts), high / len(cuts))
        return jnp.repeat(jnp.exp(draws), extent[position] // shards_of).reshape((-1,) + (1,) * (len(extent) - position - 1))

    level = one(*cuts[0])
    for cut in cuts[1:]:
        level = level * one(*cut)
    return level


def centred(stream_key, extent, deviation, bound, pieces=(), kind=jnp.bfloat16):
    level = block_levels(stream_key, extent, pieces, -0.22, 0.18) if pieces else 1.0
    drawn = jax.random.normal(stream_key, extent, jnp.float32) * deviation * level
    return jnp.minimum(jnp.maximum(drawn, -bound), bound).astype(kind)


def setup_inputs(seed: int = 0, part: int = 0) -> dict:
    streams_of = jax.random.split(jax.random.key(seed), 3)
    part_keys = jax.random.split(jax.random.fold_in(streams_of[2], part), 3)
    strain = centred(part_keys[0], (SAMPLES,), 1.0, 6.0, ((0, 16),))
    templates = centred(streams_of[1], (QUERIES, M), 1.0, 6.0, ((0, 16),))
    return {"strain": strain, "templates": templates}


EPSILON = 1e-05

def hankel(extended, width):
    count = (extended.shape[0] - width) // width
    lower = extended[:count * width].reshape(count, width)
    upper = extended[width:].reshape(count, width)
    paired = jnp.concatenate([lower, upper], axis=1)
    tiled = jnp.tile(paired, (1, width + 1))[:, :width * (2 * width + 1)]
    windows = tiled.reshape(count, width, 2 * width + 1)[:, :, :width].reshape(count * width, width)
    return (paired, windows)

def window_stats(paired, width):
    rows = jnp.arange(2 * width)[:, None]
    cols = jnp.arange(width)[None, :]
    ones_band = ((rows >= cols) & (rows < cols + width)).astype(jnp.float32)
    floats = paired.astype(jnp.float32)
    totals = jnp.dot(floats, ones_band, precision=lax.Precision.HIGHEST).reshape(-1)
    squared = jnp.dot(floats * floats, ones_band, precision=lax.Precision.HIGHEST).reshape(-1)
    win_mean = totals / width
    variance = squared / width - win_mean * win_mean
    return (win_mean, jnp.sqrt(jnp.maximum(variance, 0.0) + EPSILON))

def template_minima(windows, win_mean, win_dev, usable, templates):
    width = templates.shape[1]
    floats = templates.astype(jnp.float32)
    t_mean = lax.optimization_barrier(jnp.mean(floats, axis=1))
    t_dev = jnp.sqrt(lax.optimization_barrier(jnp.mean((floats - t_mean[:, None]) ** 2, axis=1)) + EPSILON)
    products = lax.dot_general(windows, templates, (((1,), (1,)), ((), ())), preferred_element_type=jnp.float32)
    rho = (products - width * win_mean[:, None] * t_mean[None, :]) / (width * win_dev[:, None] * t_dev[None, :])
    distance = jnp.sqrt(jnp.maximum(2.0 - 2.0 * rho, 0.0))
    distance = jnp.where(usable[:, None], distance, jnp.inf)
    return lax.optimization_barrier(jnp.min(distance, axis=0))

def reference(strain, templates):
    padded = jnp.concatenate([strain, jnp.zeros((M,), jnp.bfloat16)])

    def segment(number):
        extended = lax.dynamic_slice_in_dim(padded, number * SEG_LEN, SEG_LEN + M)
        paired, windows = hankel(extended, M)
        win_mean, win_dev = window_stats(paired, M)
        places = number * SEG_LEN + jnp.arange(SEG_LEN, dtype=jnp.int32)
        usable = places <= SEG_LEN * N_SEG - M
        return template_minima(windows, win_mean, win_dev, usable, templates)
    profile = lax.map(segment, jnp.arange(N_SEG, dtype=jnp.int32))
    return (profile, lax.optimization_barrier(jnp.min(profile, axis=0)))
```

```python
import functools

import jax
import jax.numpy as jnp
from jax import lax
from jax.experimental import pallas as pl
from jax.experimental.pallas import tpu as pltpu
from jax.sharding import PartitionSpec as P

EPSILON = 1e-05
LANES = 128
SUBLANES = 8
PACKED = 16
CENTRES = 112
TERMS = ((0, 0), (0, 1), (1, 0), (0, 2), (1, 1), (2, 0))
MESH = pl.DeviceIdType.MESH


def each(count, body):
    if count <= 16:
        for step in range(count):
            body(step)
    else:
        lax.fori_loop(0, count, lambda step, _: (body(step), 0)[1], 0)


def partner(me, step, n):
    if n & (n - 1):
        return lax.rem(me + step, n)
    other, bit = 0, 1
    while bit < n:
        mine = (me // bit) % 2
        other = other + (mine + (step // bit) % 2) % 2 * bit
        bit *= 2
    return other


def stages(chips):
    if chips == 8:
        return [[1], [2, 3], [4, 5, 6, 7]]
    return [[step] for step in range(1, chips)]


def bf16_parts(square):
    high = square.astype(jnp.bfloat16)
    return high, (square - high.astype(jnp.float32)).astype(jnp.bfloat16)


def bf16_split(value):
    parts = []
    for _ in range(3):
        parts.append(value.astype(jnp.bfloat16))
        value = value - parts[-1].astype(jnp.float32)
    return parts


def deviation(totals, squared, width):
    win_mean = totals / width
    return jnp.sqrt(jnp.maximum(squared / width - win_mean * win_mean, 0.0) + EPSILON)


def edge_sums(parts, work, rows, extra):
    source = lax.broadcasted_iota(jnp.int32, (LANES, 2 * LANES), 0)
    place = lax.broadcasted_iota(jnp.int32, (LANES, 2 * LANES), 1)
    from_place = (place < LANES) & (source >= place)
    to_place = (place >= LANES) & (source < place - LANES)
    ones = jnp.where(from_place | to_place, 1.0, 0.0).astype(jnp.bfloat16)
    both = sum(jnp.dot(part, ones, preferred_element_type=jnp.float32) for part in parts)
    first, last = both[:, :LANES], both[:, LANES:]
    work[0] = first + last
    work[1] = last
    total = first[:rows]
    for row in range(1, extra):
        total = total + work[0, pl.ds(row, rows), :]
    return total + work[1, pl.ds(extra, rows), :]


def kernel(n, width, gathers, strain_any, templates_any, both_ref,
           pair, templates_ref, halo, gathered, columns, centres, scales, leads,
           best_ref, mean_ref, norm_ref, near, hankel, work, minima, mine,
           local, pair_sems, halo_sems, t_send, t_recv, out_sems):
    me = lax.axis_index("seg")
    grp = lax.axis_index("grp")
    chip, core = me // 2, me % 2
    chips = n // 2
    sibling = chip * 2 + 1 - core
    rows = pair.shape[1]
    lanes_held = 2 * rows
    extra = width // LANES
    depth = width + LANES
    slots = gathered.shape[0]

    def scope(name):
        return jax.named_scope(name)

    def peer(step):
        down = n - 1 - step
        down = jnp.where(down <= me, down - 1, down)
        up = jnp.where(step >= me, step + 1, step)
        return jnp.where(me * 2 < n, down, up)

    fetches = [
        pltpu.make_async_copy(strain_any, pair.at[core], local.at[0]),
        pltpu.make_async_copy(templates_any, templates_ref, local.at[1]) if gathers
        else pltpu.make_async_copy(templates_any.at[core], gathered, local.at[1]),
    ]
    for fetch in fetches:
        fetch.start()
    barrier = pltpu.get_barrier_semaphore()
    each(n - 1, lambda step: pl.semaphore_signal(
        barrier, inc=1, device_id=(grp, peer(step)), device_id_type=MESH))

    with scope("fetch"):
        for fetch in fetches:
            fetch.wait()

    with scope("barrier"):
        pl.semaphore_wait(barrier, n - 1)

    pair_copy = pltpu.make_async_remote_copy(
        src_ref=pair.at[core], dst_ref=pair.at[core],
        send_sem=pair_sems.at[0], recv_sem=pair_sems.at[1],
        device_id=(grp, sibling), device_id_type=MESH)

    def halo_copy(target):
        return pltpu.make_async_remote_copy(
            src_ref=pair.at[0, pl.ds(0, PACKED)], dst_ref=halo,
            send_sem=halo_sems.at[target], recv_sem=halo_sems.at[2],
            device_id=(grp, jnp.maximum(me - 2, 0) + target), device_id_type=MESH)

    def template_copy(step):
        return pltpu.make_async_remote_copy(
            src_ref=templates_ref, dst_ref=gathered.at[chip],
            send_sem=t_send, recv_sem=t_recv.at[chip],
            device_id=(grp, partner(chip, step, chips) * 2 + core), device_id_type=MESH)

    def template_wait(start, count, sem):
        part = gathered.at[pl.ds(start, count)]
        return pltpu.make_async_remote_copy(
            src_ref=part, dst_ref=part, send_sem=t_send, recv_sem=t_recv.at[sem],
            device_id=(grp, sibling), device_id_type=MESH)

    sends_halo = (chip > 0) & (core == 0)
    gets_halo = chip < chips - 1
    with scope("tsend"):
        pair_copy.start()
        if gathers and chips > 1:
            template_copy(1).start()

        @pl.when(sends_halo)
        def _():
            for target in range(2):
                halo_copy(target).start()

        if gathers:
            for step in range(chips - 1, 1, -1):
                template_copy(step).start()
            gathered[chip] = templates_ref[...]

    lane = lax.broadcasted_iota(jnp.int32, (1, LANES), 1)

    def rows_of(slot, count):
        return pl.ds(pl.multiple_of(slot * count, count), count)

    def stagger(slot, place):
        floats = gathered[slot].astype(jnp.float32)
        t_mean = jnp.mean(floats, axis=1, keepdims=True)
        t_dev = jnp.sqrt(jnp.mean((floats - t_mean) ** 2, axis=1, keepdims=True) + EPSILON)
        means = bf16_split(t_mean)
        beyond = jnp.zeros((SUBLANES, LANES), jnp.float32)
        for j, (_, part) in enumerate(TERMS):
            beyond = jnp.where(lane == (j + 1) * PACKED, -means[part].astype(jnp.float32), beyond)
        padded = jnp.concatenate([floats, beyond], axis=1)
        padded = jnp.concatenate([padded, pltpu.roll(padded, SUBLANES, 1)], axis=0).astype(jnp.bfloat16)
        for shift in range(SUBLANES):
            leads[pl.ds((place * SUBLANES + shift) * PACKED, PACKED), :] = (
                padded if shift == 0 else pltpu.roll(padded, shift, 1))
        mean_ref[rows_of(slot, SUBLANES), :] = jnp.broadcast_to(t_mean, (SUBLANES, LANES))
        norm_ref[rows_of(slot, PACKED), :] = jnp.broadcast_to(
            jnp.concatenate([width * t_dev] * 2, axis=0), (PACKED, LANES))

    def correlate(group, place):
        best = [[jnp.full((SUBLANES, lanes_held), -jnp.inf, jnp.float32) for _ in range(2)] for _ in group]
        lead = leads[pl.ds(place * SUBLANES * PACKED, len(group) * SUBLANES * PACKED), :]
        for first in range(0, LANES, PACKED):
            samples = jnp.concatenate(
                [columns[pl.ds(first, width + PACKED), :],
                 centres[pl.ds(first * CENTRES // PACKED, CENTRES), :]], axis=0)
            products = jnp.dot(lead, samples, preferred_element_type=jnp.float32)
            for shift in range(PACKED):
                scale = scales[pl.ds(first + shift, 1), :]
                within = shift % SUBLANES * PACKED + shift // SUBLANES * SUBLANES
                for i, found in enumerate(best):
                    top = i * SUBLANES * PACKED + within
                    found[shift % 2] = jnp.maximum(
                        found[shift % 2], products[top:top + SUBLANES] * scale)
        for slot, found in zip(group, best):
            found = jnp.maximum(found[0], found[1])
            ahead = jnp.where(lane < rows - extra, found[:, rows:], -jnp.inf)
            best_ref[rows_of(slot, PACKED), :] = jnp.concatenate([found[:, :rows], ahead], axis=0)

    def work_on(group, place):
        for i, slot in enumerate(group):
            stagger(slot, place + i)
        correlate(group, place)

    with scope("pairwait"):
        pair_copy.wait_recv()

    with scope("columns"):
        strain = jnp.concatenate([pair[0].astype(jnp.float32), pair[1].astype(jnp.float32)], axis=0)
        turned = strain.T.astype(jnp.bfloat16)
        for step in range(extra + 1):
            columns[pl.ds(step * LANES, LANES), :] = (
                turned if step == 0 else pltpu.roll(turned, lanes_held - step, 1))

    with scope("stats"):
        window = lax.broadcasted_iota(jnp.int32, (LANES, depth), 0)
        sample = lax.broadcasted_iota(jnp.int32, (LANES, depth), 1)
        band = jnp.where((sample >= window) & (sample < window + width), 1.0, 0.0).astype(jnp.bfloat16)
        held = columns[...]
        wide = held.astype(jnp.float32)
        high, low = bf16_parts(wide * wide)
        totals = jnp.dot(band, held, preferred_element_type=jnp.float32)
        squared = (jnp.dot(band, high, preferred_element_type=jnp.float32)
                   + jnp.dot(band, low, preferred_element_type=jnp.float32))
        parts = bf16_split(totals)
        for first in range(0, LANES, PACKED):
            start = first * CENTRES // PACKED
            for j, (part, _) in enumerate(TERMS):
                centres[pl.ds(start + j * PACKED, PACKED), :] = parts[part][first:first + PACKED]
            centres[pl.ds(start + CENTRES - PACKED, PACKED), :] = jnp.zeros((PACKED, lanes_held), jnp.bfloat16)
        scales[...] = 1.0 / deviation(totals, squared, width)

    if gathers:
        with scope("b0"):
            work_on([chip], 0)
        place = 1
        for stage in stages(chips):
            group = [partner(chip, step, chips) for step in stage]
            with scope("w"):
                for slot in group:
                    template_wait(slot, 1, slot).wait_recv()
            with scope("b"):
                work_on(group, place)
            place += len(group)
    else:
        lax.fori_loop(0, slots, lambda slot, _: (work_on([slot], 0), 0)[1], 0)

    with scope("halo"):
        @pl.when(gets_halo)
        def _():
            halo_copy(0).wait_recv()

        @pl.when(sends_halo)
        def _():
            for target in range(2):
                halo_copy(target).wait_send()

        @pl.when(jnp.logical_not(gets_halo))
        def _():
            halo[...] = jnp.zeros_like(halo)
    with scope("edge"):
        samples = jnp.concatenate(
            [pair[1].astype(jnp.float32)[rows - extra:], halo[...].astype(jnp.float32)[:extra],
             jnp.zeros((PACKED - 2 * extra, LANES), jnp.float32)], axis=0)
        tiles = 2 * extra
        lanes = lax.broadcasted_iota(jnp.int32, (tiles, LANES), 1)
        near[:, 0, :] = samples[:tiles]
        for shift in range(1, PACKED):
            near[:, shift, :] = pltpu.roll(
                jnp.where(lanes >= shift, samples[:tiles], samples[1:tiles + 1]), LANES - shift, 1)
        span = tiles * LANES
        shifted = near[...].astype(jnp.bfloat16)
        base = jnp.concatenate([shifted[i] for i in range(tiles)], axis=1)
        for group in range(LANES // PACKED):
            turned = base if group == 0 else pltpu.roll(base, span - group * PACKED, 1)
            hankel[pl.ds(group * PACKED, PACKED), :] = turned
        block = jnp.concatenate(
            [hankel[:, pl.ds(c * LANES, extra * LANES)] for c in range(extra)], axis=0)
        e_totals = edge_sums([samples.astype(jnp.bfloat16)], work.at[0], extra, extra)
        e_squared = edge_sums(list(bf16_parts(samples * samples)), work.at[1], extra, extra)
        e_scales = 1.0 / deviation(e_totals, e_squared, width)
        templates = gathered[...].astype(jnp.float32).reshape(-1, width).astype(jnp.bfloat16)
        products = jnp.dot(templates, block, preferred_element_type=jnp.float32)
        means = mean_ref[...]
        edge = jnp.full(means.shape, -jnp.inf, jnp.float32)
        for tile in range(extra):
            score = ((products[:, tile * LANES:(tile + 1) * LANES] - e_totals[tile:tile + 1] * means)
                     * e_scales[tile:tile + 1])
            last = (lanes_held - extra + tile) * LANES + lane
            usable = gets_halo | (last <= lanes_held * LANES - width)
            edge = jnp.maximum(edge, jnp.where(usable, score, -jnp.inf))
        best = best_ref[...].reshape(slots, 2, SUBLANES, LANES)
        edge = edge.reshape(slots, SUBLANES, LANES)
        best = jnp.concatenate(
            [part for slot in range(slots)
             for part in (best[slot, 0], jnp.maximum(best[slot, 1], edge[slot]))], axis=0)
        best = best / norm_ref[...]
        rho = jnp.max(best.T, axis=0, keepdims=True)
        distance = jnp.sqrt(jnp.maximum(2.0 - 2.0 * rho, 0.0))
        mine[...] = distance
        minima[me] = distance

    def out_copy(step):
        return pltpu.make_async_remote_copy(
            src_ref=mine, dst_ref=minima.at[me],
            send_sem=out_sems.at[0], recv_sem=out_sems.at[1],
            device_id=(grp, peer(step)), device_id_type=MESH)

    with scope("osend"):
        each(n - 1, lambda step: out_copy(step).start())
    others = minima.at[pl.ds(0, n - 1)]
    arrivals = pltpu.make_async_remote_copy(
        src_ref=others, dst_ref=others, send_sem=out_sems.at[0], recv_sem=out_sems.at[1],
        device_id=(grp, sibling), device_id_type=MESH)
    with scope("sendwaits"):
        pair_copy.wait_send()
        if gathers and chips > 1:
            template_wait(0, chips - 1, 0).wait_send()
        arrivals.wait_send()
    with scope("orecv"):
        arrivals.wait_recv()

    queries = both_ref.shape[1]
    place = lax.broadcasted_iota(jnp.int32, (1, queries), 1)
    even = lax.rem(place // SUBLANES, 2) == 0

    def earlier(row):
        return pltpu.roll(row, queries - SUBLANES, 1)

    def later(row):
        return pltpu.roll(row, SUBLANES, 1)

    first, second = minima[chip * 2], minima[chip * 2 + 1]
    profile = jnp.where(
        core == 0, jnp.where(even, first, later(second)), jnp.where(even, earlier(first), second))
    found = jnp.min(minima[...].reshape(chips, 2, 1, queries), axis=0)
    overall = jnp.where(
        even, jnp.minimum(found[0], earlier(found[0])), jnp.minimum(found[1], later(found[1])))
    both_ref[...] = jnp.concatenate([profile, overall], axis=0)


def per_device(n, strain, templates):
    held, width = templates.shape
    queries = n * held
    slots = queries // PACKED
    gathers = held == SUBLANES
    if not gathers:
        templates = lax.all_gather(templates, "seg", axis=0, tiled=True)
        templates = jnp.swapaxes(templates.reshape(slots, 2, SUBLANES, width), 0, 1)
    rows = strain.shape[0] // LANES
    extra = width // LANES
    dma = pltpu.SemaphoreType.DMA
    f32, bf16 = jnp.float32, jnp.bfloat16
    both = pl.pallas_call(
        functools.partial(kernel, n, width, gathers),
        out_shape=pltpu.VMEM((2, queries), f32),
        in_specs=[pl.BlockSpec(memory_space=pl.ANY)] * 2,
        out_specs=pl.BlockSpec(memory_space=pltpu.VMEM),
        scratch_shapes=[
            pltpu.VMEM((2, rows, LANES), bf16),
            pltpu.VMEM((SUBLANES, width), bf16),
            pltpu.VMEM((PACKED, LANES), bf16),
            pltpu.VMEM((slots, SUBLANES, width), bf16),
            pltpu.VMEM((width + LANES, 2 * rows), bf16),
            pltpu.VMEM((LANES // PACKED * CENTRES, 2 * rows), bf16),
            pltpu.VMEM((LANES, 2 * rows), f32),
            pltpu.VMEM(((slots if gathers else 1) * SUBLANES * PACKED, width + LANES), bf16),
            pltpu.VMEM((queries, LANES), f32),
            pltpu.VMEM((queries // 2, LANES), f32),
            pltpu.VMEM((queries, LANES), f32),
            pltpu.VMEM((2 * extra, PACKED, LANES), f32),
            pltpu.VMEM((LANES, 2 * extra * LANES), bf16),
            pltpu.VMEM((2, 2, PACKED, LANES), f32),
            pltpu.VMEM((n, 1, queries), f32),
            pltpu.VMEM((1, queries), f32),
            dma((2,)), dma((2,)), dma((3,)), dma, dma((slots,)), dma((2,)),
        ],
        compiler_params=pltpu.CompilerParams(collective_id=0, has_side_effects=True),
    )(strain.reshape(rows, LANES), templates)
    return (both[:1], both[1])


def solution(mesh):
    in_specs = (P(("grp", "seg")), P("seg", None))
    out_specs = (P(("grp", "seg"), None), P("grp"))
    return jax.shard_map(
        functools.partial(per_device, mesh.shape["seg"]),
        mesh=mesh, in_specs=in_specs, out_specs=out_specs, check_vma=False,
    )
```

```python
import functools

import jax
import jax.numpy as jnp
from jax import lax
from jax.experimental import pallas as pl
from jax.experimental.pallas import tpu as pltpu
from jax.sharding import PartitionSpec as P

EPSILON = 1e-05
LANES = 128
SUBLANES = 8
PACKED = 16
CENTRES = 112
TERMS = ((0, 0), (0, 1), (1, 0), (0, 2), (1, 1), (2, 0))
MESH = pl.DeviceIdType.MESH


def each(count, body):
    if count <= 16:
        for step in range(count):
            body(step)
    else:
        lax.fori_loop(0, count, lambda step, _: (body(step), 0)[1], 0)


def hops(me, other):
    return abs(other // 2 - me // 2) + abs(other % 2 - me % 2)


def send_order(me, chips):
    others = [other for other in range(chips) if other != me]
    if me // 2 == 0:
        return sorted(others, key=lambda other: -hops(me, other))
    return sorted(others, key=lambda other: (other // 2, hops(me, other)))


def arrival_order(me, chips):
    def expected(other):
        entry = (chips - 2 - other // 2 * 2) * 5
        return entry + 2 * send_order(other, chips).index(me) + 9 * hops(me, other)

    return sorted((other for other in range(chips) if other != me), key=expected)


def looked_up(table, chip):
    return [sum(jnp.where(chip == me, row[step], 0) for me, row in enumerate(table)) for step in range(len(table[0]))]


def bf16_parts(square):
    high = square.astype(jnp.bfloat16)
    return high, (square - high.astype(jnp.float32)).astype(jnp.bfloat16)


def bf16_split(value):
    parts = []
    for _ in range(3):
        parts.append(value.astype(jnp.bfloat16))
        value = value - parts[-1].astype(jnp.float32)
    return parts


def deviation(totals, squared, width):
    win_mean = totals / width
    return jnp.sqrt(jnp.maximum(squared / width - win_mean * win_mean, 0.0) + EPSILON)


def edge_sums(parts, work, rows, extra):
    source = lax.broadcasted_iota(jnp.int32, (LANES, 2 * LANES), 0)
    place = lax.broadcasted_iota(jnp.int32, (LANES, 2 * LANES), 1)
    from_place = (place < LANES) & (source >= place)
    to_place = (place >= LANES) & (source < place - LANES)
    ones = jnp.where(from_place | to_place, 1.0, 0.0).astype(jnp.bfloat16)
    both = sum(jnp.dot(part, ones, preferred_element_type=jnp.float32) for part in parts)
    first, last = both[:, :LANES], both[:, LANES:]
    work[0] = first + last
    work[1] = last
    total = first[:rows]
    for row in range(1, extra):
        total = total + work[0, pl.ds(row, rows), :]
    return total + work[1, pl.ds(extra, rows), :]


def kernel(n, width, gathers, strain_any, templates_any, both_ref,
           pair, templates_ref, halo, gathered, columns, centres, scales, leads,
           best_ref, mean_ref, norm_ref, near, hankel, work, edge_stats, minima, mine,
           local, pair_sems, halo_sems, t_send, t_recv, out_sems):
    me = lax.axis_index("seg")
    grp = lax.axis_index("grp")
    chip, core = me // 2, me % 2
    chips = n // 2
    sibling = chip * 2 + 1 - core
    rows = pair.shape[1]
    lanes_held = 2 * rows
    extra = width // LANES
    depth = width + LANES
    slots = gathered.shape[0]

    def peer(step):
        down = n - 1 - step
        down = jnp.where(down <= me, down - 1, down)
        up = jnp.where(step >= me, step + 1, step)
        return jnp.where(me * 2 < n, down, up)

    fetches = [
        pltpu.make_async_copy(strain_any, pair.at[core], local.at[0]),
        pltpu.make_async_copy(templates_any, templates_ref, local.at[1]) if gathers
        else pltpu.make_async_copy(templates_any.at[core], gathered, local.at[1]),
    ]
    for fetch in fetches:
        fetch.start()
    barrier = pltpu.get_barrier_semaphore()
    each(n - 1, lambda step: pl.semaphore_signal(
        barrier, inc=1, device_id=(grp, peer(step)), device_id_type=MESH))

    for fetch in fetches:
        fetch.wait()

    pl.semaphore_wait(barrier, n - 1)

    pair_copy = pltpu.make_async_remote_copy(
        src_ref=pair.at[core], dst_ref=pair.at[core],
        send_sem=pair_sems.at[0], recv_sem=pair_sems.at[1],
        device_id=(grp, sibling), device_id_type=MESH)

    def halo_copy(target):
        return pltpu.make_async_remote_copy(
            src_ref=pair.at[0, pl.ds(0, PACKED)], dst_ref=halo,
            send_sem=halo_sems.at[target], recv_sem=halo_sems.at[2],
            device_id=(grp, jnp.maximum(chip - 1, 0) * 2 + target), device_id_type=MESH)

    def template_copy(target):
        return pltpu.make_async_remote_copy(
            src_ref=templates_ref, dst_ref=gathered.at[chip],
            send_sem=t_send, recv_sem=t_recv.at[chip],
            device_id=(grp, target * 2 + core), device_id_type=MESH)

    def template_wait(start, count, sem):
        part = gathered.at[pl.ds(start, count)]
        return pltpu.make_async_remote_copy(
            src_ref=part, dst_ref=part, send_sem=t_send, recv_sem=t_recv.at[sem],
            device_id=(grp, sibling), device_id_type=MESH)

    targets = looked_up([send_order(chip_, chips) for chip_ in range(chips)], chip) if gathers else []
    inner = chip < chips - 1
    sends_halo = (chip > 0) & (core == 0)
    no_halo = pltpu.make_async_copy(pair.at[core, pl.ds(0, PACKED)], halo, halo_sems.at[2])
    pair_copy.start()
    for target in targets[:4]:
        template_copy(target).start()

    @pl.when(sends_halo)
    def _():
        for target in range(2):
            halo_copy(target).start()

    @pl.when(jnp.logical_not(inner))
    def _():
        no_halo.start()

    for target in targets[4:]:
        template_copy(target).start()
    if gathers:
        gathered[chip] = templates_ref[...]

    lane = lax.broadcasted_iota(jnp.int32, (1, LANES), 1)

    def rows_of(slot, count):
        return pl.ds(pl.multiple_of(slot * count, count), count)

    def stagger(slot, place):
        floats = gathered[slot].astype(jnp.float32)
        t_mean = jnp.mean(floats, axis=1, keepdims=True)
        t_dev = jnp.sqrt(jnp.mean((floats - t_mean) ** 2, axis=1, keepdims=True) + EPSILON)
        means = bf16_split(t_mean)
        beyond = jnp.zeros((SUBLANES, LANES), jnp.float32)
        for j, (_, part) in enumerate(TERMS):
            beyond = jnp.where(lane == (j + 1) * PACKED, -means[part].astype(jnp.float32), beyond)
        padded = jnp.concatenate([floats, beyond], axis=1)
        padded = jnp.concatenate([padded, pltpu.roll(padded, SUBLANES, 1)], axis=0).astype(jnp.bfloat16)
        for shift in range(SUBLANES):
            leads[pl.ds((place * SUBLANES + shift) * PACKED, PACKED), :] = (
                padded if shift == 0 else pltpu.roll(padded, shift, 1))
        mean_ref[rows_of(slot, SUBLANES), :] = jnp.broadcast_to(t_mean, (SUBLANES, LANES))
        norm_ref[rows_of(slot, PACKED), :] = jnp.broadcast_to(
            jnp.concatenate([width * t_dev] * 2, axis=0), (PACKED, LANES))

    def unseen(group):
        return [[jnp.full((SUBLANES, lanes_held), -jnp.inf, jnp.float32) for _ in range(2)] for _ in group]

    def correlate(best, place, firsts):
        lead = leads[pl.ds(place * SUBLANES * PACKED, len(best) * SUBLANES * PACKED), :]
        for first in firsts:
            samples = jnp.concatenate(
                [columns[pl.ds(first, width + PACKED), :],
                 centres[pl.ds(first * CENTRES // PACKED, CENTRES), :]], axis=0)
            products = jnp.dot(lead, samples, preferred_element_type=jnp.float32)
            for shift in range(PACKED):
                scale = scales[pl.ds(first + shift, 1), :]
                within = shift % SUBLANES * PACKED + shift // SUBLANES * SUBLANES
                for i, found in enumerate(best):
                    top = i * SUBLANES * PACKED + within
                    found[shift % 2] = jnp.maximum(
                        found[shift % 2], products[top:top + SUBLANES] * scale)

    def keep(group, best):
        for slot, found in zip(group, best):
            found = jnp.maximum(found[0], found[1])
            ahead = jnp.where(lane < rows - extra, found[:, rows:], -jnp.inf)
            best_ref[rows_of(slot, PACKED), :] = jnp.concatenate([found[:, :rows], ahead], axis=0)

    every = range(0, LANES, PACKED)

    def work_on(group, place):
        for i, slot in enumerate(group):
            stagger(slot, place + i)
        best = unseen(group)
        correlate(best, place, every)
        keep(group, best)

    def await_templates(group):
        for slot in group:
            template_wait(slot, 1, slot).wait_recv()

    pair_copy.wait_recv()

    strain = jnp.concatenate([pair[0].astype(jnp.float32), pair[1].astype(jnp.float32)], axis=0)
    turned = strain.T.astype(jnp.bfloat16)
    for step in range(extra + 1):
        columns[pl.ds(step * LANES, LANES), :] = (
            turned if step == 0 else pltpu.roll(turned, lanes_held - step, 1))

    window = lax.broadcasted_iota(jnp.int32, (LANES, depth), 0)
    sample = lax.broadcasted_iota(jnp.int32, (LANES, depth), 1)
    band = jnp.where((sample >= window) & (sample < window + width), 1.0, 0.0).astype(jnp.bfloat16)
    held = columns[...]
    wide = held.astype(jnp.float32)
    high, low = bf16_parts(wide * wide)
    totals = jnp.dot(band, held, preferred_element_type=jnp.float32)
    squared = (jnp.dot(band, high, preferred_element_type=jnp.float32)
               + jnp.dot(band, low, preferred_element_type=jnp.float32))
    parts = bf16_split(totals)
    for first in range(0, LANES, PACKED):
        start = first * CENTRES // PACKED
        for j, (part, _) in enumerate(TERMS):
            centres[pl.ds(start + j * PACKED, PACKED), :] = parts[part][first:first + PACKED]
        centres[pl.ds(start + CENTRES - PACKED, PACKED), :] = jnp.zeros((PACKED, lanes_held), jnp.bfloat16)
    scales[...] = 1.0 / deviation(totals, squared, width)

    def prepare_edge():
        following = jnp.where(inner, halo[...].astype(jnp.float32)[:extra], 0.0)
        samples = jnp.concatenate(
            [pair[1].astype(jnp.float32)[rows - extra:], following,
             jnp.zeros((PACKED - 2 * extra, LANES), jnp.float32)], axis=0)
        tiles = 2 * extra
        lanes = lax.broadcasted_iota(jnp.int32, (tiles, LANES), 1)
        near[:, 0, :] = samples[:tiles]
        for shift in range(1, PACKED):
            near[:, shift, :] = pltpu.roll(
                jnp.where(lanes >= shift, samples[:tiles], samples[1:tiles + 1]), LANES - shift, 1)
        span = tiles * LANES
        shifted = near[...].astype(jnp.bfloat16)
        base = jnp.concatenate([shifted[i] for i in range(tiles)], axis=1)
        for group in range(LANES // PACKED):
            turned = base if group == 0 else pltpu.roll(base, span - group * PACKED, 1)
            hankel[pl.ds(group * PACKED, PACKED), :] = turned
        e_totals = edge_sums([samples.astype(jnp.bfloat16)], work.at[0], extra, extra)
        e_squared = edge_sums(list(bf16_parts(samples * samples)), work.at[1], extra, extra)
        e_scales = 1.0 / deviation(e_totals, e_squared, width)
        edge_stats[0] = e_totals
        edge_stats[1] = e_scales

    if gathers:
        work_on([chip], 0)
        order = looked_up([arrival_order(chip_, chips) for chip_ in range(chips)], chip)
        groups, taken = [], 0
        for count in (1, 2, 2, 2):
            groups.append((order[taken:taken + count], 1 + taken))
            taken += count
        middle = 4
        before = None
        for turn, (group, place) in enumerate(groups):
            await_templates(group)
            if turn == len(groups) - 1:
                halo_copy(0).wait_recv()
                prepare_edge()
            for i, slot in enumerate(group):
                stagger(slot, place + i)
            if before is not None:
                correlate(*before[1:], every[middle:])
                keep(*before[:2])
            best = unseen(group)
            last = turn == len(groups) - 1
            correlate(best, place, every if last else every[:middle])
            before = (group, best, place)
        keep(*before[:2])
    else:
        halo_copy(0).wait_recv()
        prepare_edge()
        lax.fori_loop(0, slots, lambda slot, _: (work_on([slot], 0), 0)[1], 0)

    block = jnp.concatenate(
        [hankel[:, pl.ds(c * LANES, extra * LANES)] for c in range(extra)], axis=0)
    e_totals, e_scales = edge_stats[0], edge_stats[1]
    templates = gathered[...].astype(jnp.float32).reshape(-1, width).astype(jnp.bfloat16)
    products = jnp.dot(templates, block, preferred_element_type=jnp.float32)
    means = mean_ref[...]
    edge = jnp.full(means.shape, -jnp.inf, jnp.float32)
    for tile in range(extra):
        score = ((products[:, tile * LANES:(tile + 1) * LANES] - e_totals[tile:tile + 1] * means)
                 * e_scales[tile:tile + 1])
        last = (lanes_held - extra + tile) * LANES + lane
        usable = inner | (last <= lanes_held * LANES - width)
        edge = jnp.maximum(edge, jnp.where(usable, score, -jnp.inf))
    best = best_ref[...].reshape(slots, 2, SUBLANES, LANES)
    edge = edge.reshape(slots, SUBLANES, LANES)
    best = jnp.concatenate(
        [part for slot in range(slots)
         for part in (best[slot, 0], jnp.maximum(best[slot, 1], edge[slot]))], axis=0)
    best = best / norm_ref[...]
    rho = jnp.max(best.T, axis=0, keepdims=True)
    distance = jnp.sqrt(jnp.maximum(2.0 - 2.0 * rho, 0.0))
    mine[...] = distance
    minima[me] = distance

    def out_copy(step):
        return pltpu.make_async_remote_copy(
            src_ref=mine, dst_ref=minima.at[me],
            send_sem=out_sems.at[0], recv_sem=out_sems.at[1],
            device_id=(grp, peer(step)), device_id_type=MESH)

    each(n - 1, lambda step: out_copy(step).start())
    others = minima.at[pl.ds(0, n - 1)]
    arrivals = pltpu.make_async_remote_copy(
        src_ref=others, dst_ref=others, send_sem=out_sems.at[0], recv_sem=out_sems.at[1],
        device_id=(grp, sibling), device_id_type=MESH)
    pair_copy.wait_send()
    if gathers and chips > 1:
        template_wait(0, chips - 1, 0).wait_send()
    arrivals.wait_send()

    @pl.when(sends_halo)
    def _():
        for target in range(2):
            halo_copy(target).wait_send()

    arrivals.wait_recv()

    queries = both_ref.shape[1]
    place = lax.broadcasted_iota(jnp.int32, (1, queries), 1)
    even = lax.rem(place // SUBLANES, 2) == 0

    def earlier(row):
        return pltpu.roll(row, queries - SUBLANES, 1)

    def later(row):
        return pltpu.roll(row, SUBLANES, 1)

    first, second = minima[chip * 2], minima[chip * 2 + 1]
    profile = jnp.where(
        core == 0, jnp.where(even, first, later(second)), jnp.where(even, earlier(first), second))
    found = jnp.min(minima[...].reshape(chips, 2, 1, queries), axis=0)
    overall = jnp.where(
        even, jnp.minimum(found[0], earlier(found[0])), jnp.minimum(found[1], later(found[1])))
    both_ref[...] = jnp.concatenate([profile, overall], axis=0)


def per_device(n, strain, templates):
    held, width = templates.shape
    queries = n * held
    slots = queries // PACKED
    gathers = held == SUBLANES
    if not gathers:
        templates = lax.all_gather(templates, "seg", axis=0, tiled=True)
        templates = jnp.swapaxes(templates.reshape(slots, 2, SUBLANES, width), 0, 1)
    rows = strain.shape[0] // LANES
    extra = width // LANES
    dma = pltpu.SemaphoreType.DMA
    f32, bf16 = jnp.float32, jnp.bfloat16
    both = pl.pallas_call(
        functools.partial(kernel, n, width, gathers),
        out_shape=pltpu.VMEM((2, queries), f32),
        in_specs=[pl.BlockSpec(memory_space=pl.ANY)] * 2,
        out_specs=pl.BlockSpec(memory_space=pltpu.VMEM),
        scratch_shapes=[
            pltpu.VMEM((2, rows, LANES), bf16),
            pltpu.VMEM((SUBLANES, width), bf16),
            pltpu.VMEM((PACKED, LANES), bf16),
            pltpu.VMEM((slots, SUBLANES, width), bf16),
            pltpu.VMEM((width + LANES, 2 * rows), bf16),
            pltpu.VMEM((LANES // PACKED * CENTRES, 2 * rows), bf16),
            pltpu.VMEM((LANES, 2 * rows), f32),
            pltpu.VMEM(((slots if gathers else 1) * SUBLANES * PACKED, width + LANES), bf16),
            pltpu.VMEM((queries, LANES), f32),
            pltpu.VMEM((queries // 2, LANES), f32),
            pltpu.VMEM((queries, LANES), f32),
            pltpu.VMEM((2 * extra, PACKED, LANES), f32),
            pltpu.VMEM((LANES, 2 * extra * LANES), bf16),
            pltpu.VMEM((2, 2, PACKED, LANES), f32),
            pltpu.VMEM((2, extra, LANES), f32),
            pltpu.VMEM((n, 1, queries), f32),
            pltpu.VMEM((1, queries), f32),
            dma((2,)), dma((2,)), dma((3,)), dma, dma((slots,)), dma((2,)),
        ],
        compiler_params=pltpu.CompilerParams(collective_id=0, has_side_effects=True),
    )(strain.reshape(rows, LANES), templates)
    return (both[:1], both[1])


def solution(mesh):
    in_specs = (P(("grp", "seg")), P("seg", None))
    out_specs = (P(("grp", "seg"), None), P("grp"))
    return jax.shard_map(
        functools.partial(per_device, mesh.shape["seg"]),
        mesh=mesh, in_specs=in_specs, out_specs=out_specs, check_vma=False,
    )
```

```python
import functools

import jax
import jax.numpy as jnp
from jax import lax
from jax.experimental import pallas as pl
from jax.experimental.pallas import tpu as pltpu
from jax.sharding import PartitionSpec as P

EPSILON = 1e-05
LANES = 128
SUBLANES = 8
PACKED = 16
CENTRES = 112
FIRST_GROUPS = (2, 1)
TERMS = ((0, 0), (0, 1), (1, 0), (0, 2), (1, 1), (2, 0))
MESH = pl.DeviceIdType.MESH


def each(count, body):
    if count <= 16:
        for step in range(count):
            body(step)
    else:
        lax.fori_loop(0, count, lambda step, _: (body(step), 0)[1], 0)


def hops(me, other):
    return abs(other // 2 - me // 2) + abs(other % 2 - me % 2)


def send_order(me, chips):
    others = [other for other in range(chips) if other != me]
    if me // 2 == (chips - 1) // 2:
        return sorted(others, key=lambda other: (other // 2 != me // 2, other // 2, hops(me, other)))
    return sorted(others, key=lambda other: (-(other // 2), -hops(me, other)))


def arrival_order(me, chips):
    def expected(other):
        entry = (chips - 2 - other // 2 * 2) * 5
        return entry + 2 * send_order(other, chips).index(me) + 9 * hops(me, other)

    return sorted((other for other in range(chips) if other != me), key=expected)


def looked_up(table, chip):
    return [sum(jnp.where(chip == me, row[step], 0) for me, row in enumerate(table)) for step in range(len(table[0]))]


def bf16_parts(square):
    high = square.astype(jnp.bfloat16)
    return high, (square - high.astype(jnp.float32)).astype(jnp.bfloat16)


def bf16_split(value):
    parts = []
    for _ in range(3):
        parts.append(value.astype(jnp.bfloat16))
        value = value - parts[-1].astype(jnp.float32)
    return parts


def deviation(totals, squared, width):
    win_mean = totals / width
    return jnp.sqrt(jnp.maximum(squared / width - win_mean * win_mean, 0.0) + EPSILON)


def edge_sums(parts, work, rows, extra):
    source = lax.broadcasted_iota(jnp.int32, (LANES, 2 * LANES), 0)
    place = lax.broadcasted_iota(jnp.int32, (LANES, 2 * LANES), 1)
    from_place = (place < LANES) & (source >= place)
    to_place = (place >= LANES) & (source < place - LANES)
    ones = jnp.where(from_place | to_place, 1.0, 0.0).astype(jnp.bfloat16)
    both = sum(jnp.dot(part, ones, preferred_element_type=jnp.float32) for part in parts)
    first, last = both[:, :LANES], both[:, LANES:]
    work[0] = first + last
    work[1] = last
    total = first[:rows]
    for row in range(1, extra):
        total = total + work[0, pl.ds(row, rows), :]
    return total + work[1, pl.ds(extra, rows), :]


def kernel(n, width, gathers, strain_any, templates_any, both_ref,
           pair, templates_ref, halo, gathered, columns, centres, scales, leads,
           best_ref, mean_ref, norm_ref, near, hankel, work, edge_stats, minima, mine,
           local, pair_sems, halo_sems, t_send, t_recv, out_sems):
    me = lax.axis_index("seg")
    grp = lax.axis_index("grp")
    chip, core = me // 2, me % 2
    chips = n // 2
    sibling = chip * 2 + 1 - core
    rows = pair.shape[1]
    lanes_held = 2 * rows
    extra = width // LANES
    depth = width + LANES
    slots = gathered.shape[0]

    def peer(step):
        down = n - 1 - step
        down = jnp.where(down <= me, down - 1, down)
        up = jnp.where(step >= me, step + 1, step)
        return jnp.where(me * 2 < n, down, up)

    fetches = [
        pltpu.make_async_copy(strain_any, pair.at[core], local.at[0]),
        pltpu.make_async_copy(templates_any, templates_ref, local.at[1]) if gathers
        else pltpu.make_async_copy(templates_any.at[core], gathered, local.at[1]),
    ]
    for fetch in fetches:
        fetch.start()
    barrier = pltpu.get_barrier_semaphore()
    each(n - 1, lambda step: pl.semaphore_signal(
        barrier, inc=1, device_id=(grp, peer(step)), device_id_type=MESH))

    for fetch in fetches:
        fetch.wait()

    pl.semaphore_wait(barrier, n - 1)

    pair_copy = pltpu.make_async_remote_copy(
        src_ref=pair.at[core], dst_ref=pair.at[core],
        send_sem=pair_sems.at[0], recv_sem=pair_sems.at[1],
        device_id=(grp, sibling), device_id_type=MESH)

    def halo_copy(target):
        return pltpu.make_async_remote_copy(
            src_ref=pair.at[0, pl.ds(0, PACKED)], dst_ref=halo,
            send_sem=halo_sems.at[target], recv_sem=halo_sems.at[2],
            device_id=(grp, jnp.maximum(chip - 1, 0) * 2 + target), device_id_type=MESH)

    def template_copy(target):
        return pltpu.make_async_remote_copy(
            src_ref=templates_ref, dst_ref=gathered.at[chip],
            send_sem=t_send, recv_sem=t_recv.at[chip],
            device_id=(grp, target * 2 + core), device_id_type=MESH)

    def template_wait(start, count, sem):
        part = gathered.at[pl.ds(start, count)]
        return pltpu.make_async_remote_copy(
            src_ref=part, dst_ref=part, send_sem=t_send, recv_sem=t_recv.at[sem],
            device_id=(grp, sibling), device_id_type=MESH)

    targets = looked_up([send_order(chip_, chips) for chip_ in range(chips)], chip) if gathers else []
    inner = chip < chips - 1
    sends_halo = (chip > 0) & (core == 0)
    no_halo = pltpu.make_async_copy(pair.at[core, pl.ds(0, PACKED)], halo, halo_sems.at[2])
    pair_copy.start()
    for target in targets[:4]:
        template_copy(target).start()

    @pl.when(sends_halo)
    def _():
        for target in range(2):
            halo_copy(target).start()

    @pl.when(jnp.logical_not(inner))
    def _():
        no_halo.start()

    for target in targets[4:]:
        template_copy(target).start()
    if gathers:
        gathered[chip] = templates_ref[...]

    lane = lax.broadcasted_iota(jnp.int32, (1, LANES), 1)

    def rows_of(slot, count):
        return pl.ds(pl.multiple_of(slot * count, count), count)

    def stagger(slot, place):
        floats = gathered[slot].astype(jnp.float32)
        t_mean = jnp.mean(floats, axis=1, keepdims=True)
        t_dev = jnp.sqrt(jnp.mean((floats - t_mean) ** 2, axis=1, keepdims=True) + EPSILON)
        means = bf16_split(t_mean)
        beyond = jnp.zeros((SUBLANES, LANES), jnp.float32)
        for j, (_, part) in enumerate(TERMS):
            beyond = jnp.where(lane == (j + 1) * PACKED, -means[part].astype(jnp.float32), beyond)
        padded = jnp.concatenate([floats, beyond], axis=1)
        padded = jnp.concatenate([padded, pltpu.roll(padded, SUBLANES, 1)], axis=0).astype(jnp.bfloat16)
        for shift in range(SUBLANES):
            leads[pl.ds((place * SUBLANES + shift) * PACKED, PACKED), :] = (
                padded if shift == 0 else pltpu.roll(padded, shift, 1))
        mean_ref[rows_of(slot, SUBLANES), :] = jnp.broadcast_to(t_mean, (SUBLANES, LANES))
        norm_ref[rows_of(slot, PACKED), :] = jnp.broadcast_to(
            jnp.concatenate([width * t_dev] * 2, axis=0), (PACKED, LANES))

    def unseen(group):
        return [[jnp.full((SUBLANES, lanes_held), -jnp.inf, jnp.float32) for _ in range(2)] for _ in group]

    def correlate(best, place, firsts):
        lead = leads[pl.ds(place * SUBLANES * PACKED, len(best) * SUBLANES * PACKED), :]
        for first in firsts:
            samples = jnp.concatenate(
                [columns[pl.ds(first, width + PACKED), :],
                 centres[pl.ds(first * CENTRES // PACKED, CENTRES), :]], axis=0)
            products = jnp.dot(lead, samples, preferred_element_type=jnp.float32)
            for shift in range(PACKED):
                scale = scales[pl.ds(first + shift, 1), :]
                within = shift % SUBLANES * PACKED + shift // SUBLANES * SUBLANES
                for i, found in enumerate(best):
                    top = i * SUBLANES * PACKED + within
                    found[shift % 2] = jnp.maximum(
                        found[shift % 2], products[top:top + SUBLANES] * scale)

    def keep(group, best):
        for slot, found in zip(group, best):
            found = jnp.maximum(found[0], found[1])
            ahead = jnp.where(lane < rows - extra, found[:, rows:], -jnp.inf)
            best_ref[rows_of(slot, PACKED), :] = jnp.concatenate([found[:, :rows], ahead], axis=0)

    every = range(0, LANES, PACKED)

    def work_on(group, place):
        for i, slot in enumerate(group):
            stagger(slot, place + i)
        best = unseen(group)
        correlate(best, place, every)
        keep(group, best)

    def await_templates(group):
        for slot in group:
            template_wait(slot, 1, slot).wait_recv()

    pair_copy.wait_recv()

    strain = jnp.concatenate([pair[0].astype(jnp.float32), pair[1].astype(jnp.float32)], axis=0)
    turned = strain.T.astype(jnp.bfloat16)
    for step in range(extra + 1):
        columns[pl.ds(step * LANES, LANES), :] = (
            turned if step == 0 else pltpu.roll(turned, lanes_held - step, 1))

    window = lax.broadcasted_iota(jnp.int32, (LANES, depth), 0)
    sample = lax.broadcasted_iota(jnp.int32, (LANES, depth), 1)
    band = jnp.where((sample >= window) & (sample < window + width), 1.0, 0.0).astype(jnp.bfloat16)
    held = columns[...]
    wide = held.astype(jnp.float32)
    high, low = bf16_parts(wide * wide)
    totals = jnp.dot(band, held, preferred_element_type=jnp.float32)
    squared = (jnp.dot(band, high, preferred_element_type=jnp.float32)
               + jnp.dot(band, low, preferred_element_type=jnp.float32))
    parts = bf16_split(totals)
    for first in range(0, LANES, PACKED):
        start = first * CENTRES // PACKED
        for j, (part, _) in enumerate(TERMS):
            centres[pl.ds(start + j * PACKED, PACKED), :] = parts[part][first:first + PACKED]
        centres[pl.ds(start + CENTRES - PACKED, PACKED), :] = jnp.zeros((PACKED, lanes_held), jnp.bfloat16)
    scales[...] = 1.0 / deviation(totals, squared, width)

    def prepare_edge():
        following = jnp.where(inner, halo[...].astype(jnp.float32)[:extra], 0.0)
        samples = jnp.concatenate(
            [pair[1].astype(jnp.float32)[rows - extra:], following,
             jnp.zeros((PACKED - 2 * extra, LANES), jnp.float32)], axis=0)
        tiles = 2 * extra
        lanes = lax.broadcasted_iota(jnp.int32, (tiles, LANES), 1)
        near[:, 0, :] = samples[:tiles]
        for shift in range(1, PACKED):
            near[:, shift, :] = pltpu.roll(
                jnp.where(lanes >= shift, samples[:tiles], samples[1:tiles + 1]), LANES - shift, 1)
        span = tiles * LANES
        shifted = near[...].astype(jnp.bfloat16)
        base = jnp.concatenate([shifted[i] for i in range(tiles)], axis=1)
        for group in range(LANES // PACKED):
            turned = base if group == 0 else pltpu.roll(base, span - group * PACKED, 1)
            hankel[pl.ds(group * PACKED, PACKED), :] = turned
        e_totals = edge_sums([samples.astype(jnp.bfloat16)], work.at[0], extra, extra)
        e_squared = edge_sums(list(bf16_parts(samples * samples)), work.at[1], extra, extra)
        e_scales = 1.0 / deviation(e_totals, e_squared, width)
        edge_stats[0] = e_totals
        edge_stats[1] = e_scales

    if gathers:
        work_on([chip], 0)
        order = looked_up([arrival_order(chip_, chips) for chip_ in range(chips)], chip)
        groups, taken = [], 0
        while taken < len(order):
            count = FIRST_GROUPS[len(groups)] if len(groups) < len(FIRST_GROUPS) else 2
            groups.append((order[taken:taken + count], 1 + taken))
            taken += count
        middle = len(every) // 2
        before = None
        for turn, (group, place) in enumerate(groups):
            await_templates(group)
            if turn == len(groups) - 1:
                halo_copy(0).wait_recv()
                prepare_edge()
            for i, slot in enumerate(group):
                stagger(slot, place + i)
            if before is not None:
                correlate(*before[1:], every[middle:])
                keep(*before[:2])
            best = unseen(group)
            last = turn == len(groups) - 1
            correlate(best, place, every if last else every[:middle])
            before = (group, best, place)
        keep(*before[:2])
    else:
        halo_copy(0).wait_recv()
        prepare_edge()
        lax.fori_loop(0, slots, lambda slot, _: (work_on([slot], 0), 0)[1], 0)

    block = jnp.concatenate(
        [hankel[:, pl.ds(c * LANES, extra * LANES)] for c in range(extra)], axis=0)
    e_totals, e_scales = edge_stats[0], edge_stats[1]
    templates = gathered[...].astype(jnp.float32).reshape(-1, width).astype(jnp.bfloat16)
    products = jnp.dot(templates, block, preferred_element_type=jnp.float32)
    means = mean_ref[...]
    edge = jnp.full(means.shape, -jnp.inf, jnp.float32)
    for tile in range(extra):
        score = ((products[:, tile * LANES:(tile + 1) * LANES] - e_totals[tile:tile + 1] * means)
                 * e_scales[tile:tile + 1])
        last = (lanes_held - extra + tile) * LANES + lane
        usable = inner | (last <= lanes_held * LANES - width)
        edge = jnp.maximum(edge, jnp.where(usable, score, -jnp.inf))
    best = best_ref[...].reshape(slots, 2, SUBLANES, LANES)
    edge = edge.reshape(slots, SUBLANES, LANES)
    best = jnp.concatenate(
        [part for slot in range(slots)
         for part in (best[slot, 0], jnp.maximum(best[slot, 1], edge[slot]))], axis=0)
    best = best / norm_ref[...]
    rho = jnp.max(best.T, axis=0, keepdims=True)
    distance = jnp.sqrt(jnp.maximum(2.0 - 2.0 * rho, 0.0))
    mine[...] = distance
    minima[me] = distance

    def out_copy(step):
        return pltpu.make_async_remote_copy(
            src_ref=mine, dst_ref=minima.at[me],
            send_sem=out_sems.at[0], recv_sem=out_sems.at[1],
            device_id=(grp, peer(step)), device_id_type=MESH)

    each(n - 1, lambda step: out_copy(step).start())
    others = minima.at[pl.ds(0, n - 1)]
    arrivals = pltpu.make_async_remote_copy(
        src_ref=others, dst_ref=others, send_sem=out_sems.at[0], recv_sem=out_sems.at[1],
        device_id=(grp, sibling), device_id_type=MESH)
    pair_copy.wait_send()
    if gathers and chips > 1:
        template_wait(0, chips - 1, 0).wait_send()
    arrivals.wait_send()

    @pl.when(sends_halo)
    def _():
        for target in range(2):
            halo_copy(target).wait_send()

    arrivals.wait_recv()

    queries = both_ref.shape[1]
    place = lax.broadcasted_iota(jnp.int32, (1, queries), 1)
    even = lax.rem(place // SUBLANES, 2) == 0

    def earlier(row):
        return pltpu.roll(row, queries - SUBLANES, 1)

    def later(row):
        return pltpu.roll(row, SUBLANES, 1)

    first, second = minima[chip * 2], minima[chip * 2 + 1]
    profile = jnp.where(
        core == 0, jnp.where(even, first, later(second)), jnp.where(even, earlier(first), second))
    found = jnp.min(minima[...].reshape(chips, 2, 1, queries), axis=0)
    overall = jnp.where(
        even, jnp.minimum(found[0], earlier(found[0])), jnp.minimum(found[1], later(found[1])))
    both_ref[...] = jnp.concatenate([profile, overall], axis=0)


def per_device(n, strain, templates):
    held, width = templates.shape
    queries = n * held
    slots = queries // PACKED
    gathers = held == SUBLANES
    if not gathers:
        templates = lax.all_gather(templates, "seg", axis=0, tiled=True)
        templates = jnp.swapaxes(templates.reshape(slots, 2, SUBLANES, width), 0, 1)
    rows = strain.shape[0] // LANES
    extra = width // LANES
    dma = pltpu.SemaphoreType.DMA
    f32, bf16 = jnp.float32, jnp.bfloat16
    both = pl.pallas_call(
        functools.partial(kernel, n, width, gathers),
        out_shape=pltpu.VMEM((2, queries), f32),
        in_specs=[pl.BlockSpec(memory_space=pl.ANY)] * 2,
        out_specs=pl.BlockSpec(memory_space=pltpu.VMEM),
        scratch_shapes=[
            pltpu.VMEM((2, rows, LANES), bf16),
            pltpu.VMEM((SUBLANES, width), bf16),
            pltpu.VMEM((PACKED, LANES), bf16),
            pltpu.VMEM((slots, SUBLANES, width), bf16),
            pltpu.VMEM((width + LANES, 2 * rows), bf16),
            pltpu.VMEM((LANES // PACKED * CENTRES, 2 * rows), bf16),
            pltpu.VMEM((LANES, 2 * rows), f32),
            pltpu.VMEM(((slots if gathers else 1) * SUBLANES * PACKED, width + LANES), bf16),
            pltpu.VMEM((queries, LANES), f32),
            pltpu.VMEM((queries // 2, LANES), f32),
            pltpu.VMEM((queries, LANES), f32),
            pltpu.VMEM((2 * extra, PACKED, LANES), f32),
            pltpu.VMEM((LANES, 2 * extra * LANES), bf16),
            pltpu.VMEM((2, 2, PACKED, LANES), f32),
            pltpu.VMEM((2, extra, LANES), f32),
            pltpu.VMEM((n, 1, queries), f32),
            pltpu.VMEM((1, queries), f32),
            dma((2,)), dma((2,)), dma((3,)), dma, dma((slots,)), dma((2,)),
        ],
        compiler_params=pltpu.CompilerParams(collective_id=0, has_side_effects=True),
    )(strain.reshape(rows, LANES), templates)
    return (both[:1], both[1])


def solution(mesh):
    in_specs = (P(("grp", "seg")), P("seg", None))
    out_specs = (P(("grp", "seg"), None), P("grp"))
    return jax.shard_map(
        functools.partial(per_device, mesh.shape["seg"]),
        mesh=mesh, in_specs=in_specs, out_specs=out_specs, check_vma=False,
    )
```

```python
import functools

import jax
import jax.numpy as jnp
from jax import lax
from jax.experimental import pallas as pl
from jax.experimental.pallas import tpu as pltpu
from jax.sharding import PartitionSpec as P

EPSILON = 1e-05
LANES = 128
SUBLANES = 8
PACKED = 16
CENTRES = 112
FIRST_GROUPS = (2, 1)
TERMS = ((0, 0), (0, 1), (1, 0), (0, 2), (1, 1), (2, 0))
MESH = pl.DeviceIdType.MESH


def each(count, body):
    if count <= 16:
        for step in range(count):
            body(step)
    else:
        lax.fori_loop(0, count, lambda step, _: (body(step), 0)[1], 0)


def hops(me, other):
    return abs(other // 2 - me // 2) + abs(other % 2 - me % 2)


def send_order(me, chips):
    others = [other for other in range(chips) if other != me]
    if me // 2 == (chips - 1) // 2:
        return sorted(others, key=lambda other: (other // 2 != me // 2, other // 2, hops(me, other)))
    return sorted(others, key=lambda other: (-(other // 2), -hops(me, other)))


def arrival_order(me, chips):
    def expected(other):
        entry = (chips - 2 - other // 2 * 2) * 5
        return entry + 2 * send_order(other, chips).index(me) + 9 * hops(me, other)

    return sorted((other for other in range(chips) if other != me), key=expected)


def looked_up(table, chip):
    return [sum(jnp.where(chip == me, row[step], 0) for me, row in enumerate(table)) for step in range(len(table[0]))]


def bf16_parts(square):
    high = square.astype(jnp.bfloat16)
    return high, (square - high.astype(jnp.float32)).astype(jnp.bfloat16)


def bf16_split(value):
    parts = []
    for _ in range(3):
        parts.append(value.astype(jnp.bfloat16))
        value = value - parts[-1].astype(jnp.float32)
    return parts


def deviation(totals, squared, width):
    win_mean = totals / width
    return jnp.sqrt(jnp.maximum(squared / width - win_mean * win_mean, 0.0) + EPSILON)


def edge_sums(parts, work, rows, extra):
    source = lax.broadcasted_iota(jnp.int32, (LANES, 2 * LANES), 0)
    place = lax.broadcasted_iota(jnp.int32, (LANES, 2 * LANES), 1)
    from_place = (place < LANES) & (source >= place)
    to_place = (place >= LANES) & (source < place - LANES)
    ones = jnp.where(from_place | to_place, 1.0, 0.0).astype(jnp.bfloat16)
    both = sum(jnp.dot(part, ones, preferred_element_type=jnp.float32) for part in parts)
    first, last = both[:, :LANES], both[:, LANES:]
    work[0] = first + last
    work[1] = last
    total = first[:rows]
    for row in range(1, extra):
        total = total + work[0, pl.ds(row, rows), :]
    return total + work[1, pl.ds(extra, rows), :]


def kernel(n, width, gathers, strain_any, templates_any, both_ref,
           pair, templates_ref, halo, gathered, columns, centres, scales, leads,
           best_ref, mean_ref, norm_ref, near, hankel, work, edge_stats, minima, mine,
           local, pair_sems, halo_sems, t_send, t_recv, out_sems):
    me = lax.axis_index("seg")
    grp = lax.axis_index("grp")
    chip, core = me // 2, me % 2
    chips = n // 2
    sibling = chip * 2 + 1 - core
    rows = pair.shape[1]
    lanes_held = 2 * rows
    extra = width // LANES
    depth = width + LANES
    slots = gathered.shape[0]

    def peer(step):
        down = n - 1 - step
        down = jnp.where(down <= me, down - 1, down)
        up = jnp.where(step >= me, step + 1, step)
        return jnp.where(me * 2 < n, down, up)

    fetches = [
        pltpu.make_async_copy(strain_any, pair.at[core], local.at[0]),
        pltpu.make_async_copy(templates_any, templates_ref, local.at[1]) if gathers
        else pltpu.make_async_copy(templates_any.at[core], gathered, local.at[1]),
    ]
    for fetch in fetches:
        fetch.start()
    barrier = pltpu.get_barrier_semaphore()
    each(n - 1, lambda step: pl.semaphore_signal(
        barrier, inc=1, device_id=(grp, peer(step)), device_id_type=MESH))

    for fetch in fetches:
        fetch.wait()

    pl.semaphore_wait(barrier, n - 1)

    pair_copy = pltpu.make_async_remote_copy(
        src_ref=pair.at[core], dst_ref=pair.at[core],
        send_sem=pair_sems.at[0], recv_sem=pair_sems.at[1],
        device_id=(grp, sibling), device_id_type=MESH)

    def halo_copy(target):
        return pltpu.make_async_remote_copy(
            src_ref=pair.at[0, pl.ds(0, PACKED)], dst_ref=halo,
            send_sem=halo_sems.at[target], recv_sem=halo_sems.at[2],
            device_id=(grp, jnp.maximum(chip - 1, 0) * 2 + target), device_id_type=MESH)

    def template_copy(target):
        return pltpu.make_async_remote_copy(
            src_ref=templates_ref, dst_ref=gathered.at[chip],
            send_sem=t_send, recv_sem=t_recv.at[chip],
            device_id=(grp, target * 2 + core), device_id_type=MESH)

    def template_wait(start, count, sem):
        part = gathered.at[pl.ds(start, count)]
        return pltpu.make_async_remote_copy(
            src_ref=part, dst_ref=part, send_sem=t_send, recv_sem=t_recv.at[sem],
            device_id=(grp, sibling), device_id_type=MESH)

    targets = looked_up([send_order(chip_, chips) for chip_ in range(chips)], chip) if gathers else []
    inner = chip < chips - 1
    sends_halo = (chip > 0) & (core == 0)
    no_halo = pltpu.make_async_copy(pair.at[core, pl.ds(0, PACKED)], halo, halo_sems.at[2])
    pair_copy.start()
    for target in targets[:4]:
        template_copy(target).start()

    @pl.when(sends_halo)
    def _():
        for target in range(2):
            halo_copy(target).start()

    @pl.when(jnp.logical_not(inner))
    def _():
        no_halo.start()

    for target in targets[4:]:
        template_copy(target).start()
    if gathers:
        gathered[chip] = templates_ref[...]

    lane = lax.broadcasted_iota(jnp.int32, (1, LANES), 1)

    def rows_of(slot, count):
        return pl.ds(pl.multiple_of(slot * count, count), count)

    def stagger(slot, place):
        floats = gathered[slot].astype(jnp.float32)
        t_mean = jnp.mean(floats, axis=1, keepdims=True)
        t_dev = jnp.sqrt(jnp.mean((floats - t_mean) ** 2, axis=1, keepdims=True) + EPSILON)
        means = bf16_split(t_mean)
        beyond = jnp.zeros((SUBLANES, LANES), jnp.float32)
        for j, (_, part) in enumerate(TERMS):
            beyond = jnp.where(lane == (j + 1) * PACKED, -means[part].astype(jnp.float32), beyond)
        padded = jnp.concatenate([floats, beyond], axis=1)
        padded = jnp.concatenate([padded, pltpu.roll(padded, SUBLANES, 1)], axis=0).astype(jnp.bfloat16)
        for shift in range(SUBLANES):
            leads[pl.ds((place * SUBLANES + shift) * PACKED, PACKED), :] = (
                padded if shift == 0 else pltpu.roll(padded, shift, 1))
        mean_ref[rows_of(slot, SUBLANES), :] = jnp.broadcast_to(t_mean, (SUBLANES, LANES))
        norm_ref[rows_of(slot, PACKED), :] = jnp.broadcast_to(
            jnp.concatenate([width * t_dev] * 2, axis=0), (PACKED, LANES))

    def unseen(group):
        return [[jnp.full((SUBLANES, lanes_held), -jnp.inf, jnp.float32) for _ in range(2)] for _ in group]

    def correlate(best, place, firsts):
        lead = leads[pl.ds(place * SUBLANES * PACKED, len(best) * SUBLANES * PACKED), :]
        for first in firsts:
            samples = jnp.concatenate(
                [columns[pl.ds(first, width + PACKED), :],
                 centres[pl.ds(first * CENTRES // PACKED, CENTRES), :]], axis=0)
            products = jnp.dot(lead, samples, preferred_element_type=jnp.float32)
            for shift in range(PACKED):
                scale = scales[pl.ds(first + shift, 1), :]
                within = shift % SUBLANES * PACKED + shift // SUBLANES * SUBLANES
                for i, found in enumerate(best):
                    top = i * SUBLANES * PACKED + within
                    found[shift % 2] = jnp.maximum(
                        found[shift % 2], products[top:top + SUBLANES] * scale)

    def keep(group, best):
        for slot, found in zip(group, best):
            found = jnp.maximum(found[0], found[1])
            ahead = jnp.where(lane < rows - extra, found[:, rows:], -jnp.inf)
            best_ref[rows_of(slot, PACKED), :] = jnp.concatenate([found[:, :rows], ahead], axis=0)

    every = range(0, LANES, PACKED)

    def work_on(group, place):
        for i, slot in enumerate(group):
            stagger(slot, place + i)
        best = unseen(group)
        correlate(best, place, every)
        keep(group, best)

    def await_templates(group):
        for slot in group:
            template_wait(slot, 1, slot).wait_recv()

    pair_copy.wait_recv()

    strain = jnp.concatenate([pair[0].astype(jnp.float32), pair[1].astype(jnp.float32)], axis=0)
    turned = strain.T.astype(jnp.bfloat16)
    for step in range(extra + 1):
        columns[pl.ds(step * LANES, LANES), :] = (
            turned if step == 0 else pltpu.roll(turned, lanes_held - step, 1))

    window = lax.broadcasted_iota(jnp.int32, (LANES, depth), 0)
    sample = lax.broadcasted_iota(jnp.int32, (LANES, depth), 1)
    band = jnp.where((sample >= window) & (sample < window + width), 1.0, 0.0).astype(jnp.bfloat16)
    held = columns[...]
    wide = held.astype(jnp.float32)
    high, low = bf16_parts(wide * wide)
    totals = jnp.dot(band, held, preferred_element_type=jnp.float32)
    squared = (jnp.dot(band, high, preferred_element_type=jnp.float32)
               + jnp.dot(band, low, preferred_element_type=jnp.float32))
    parts = bf16_split(totals)
    for first in range(0, LANES, PACKED):
        start = first * CENTRES // PACKED
        for j, (part, _) in enumerate(TERMS):
            centres[pl.ds(start + j * PACKED, PACKED), :] = parts[part][first:first + PACKED]
        centres[pl.ds(start + CENTRES - PACKED, PACKED), :] = jnp.zeros((PACKED, lanes_held), jnp.bfloat16)
    scales[...] = 1.0 / deviation(totals, squared, width)

    def prepare_edge():
        following = jnp.where(inner, halo[...].astype(jnp.float32)[:extra], 0.0)
        samples = jnp.concatenate(
            [pair[1].astype(jnp.float32)[rows - extra:], following,
             jnp.zeros((PACKED - 2 * extra, LANES), jnp.float32)], axis=0)
        tiles = 2 * extra
        lanes = lax.broadcasted_iota(jnp.int32, (tiles, LANES), 1)
        near[:, 0, :] = samples[:tiles]
        for shift in range(1, PACKED):
            near[:, shift, :] = pltpu.roll(
                jnp.where(lanes >= shift, samples[:tiles], samples[1:tiles + 1]), LANES - shift, 1)
        span = tiles * LANES
        shifted = near[...].astype(jnp.bfloat16)
        base = jnp.concatenate([shifted[i] for i in range(tiles)], axis=1)
        for group in range(LANES // PACKED):
            turned = base if group == 0 else pltpu.roll(base, span - group * PACKED, 1)
            hankel[pl.ds(group * PACKED, PACKED), :] = turned
        e_totals = edge_sums([samples.astype(jnp.bfloat16)], work.at[0], extra, extra)
        e_squared = edge_sums(list(bf16_parts(samples * samples)), work.at[1], extra, extra)
        e_scales = 1.0 / deviation(e_totals, e_squared, width)
        edge_stats[0] = e_totals
        edge_stats[1] = e_scales

    if gathers:
        work_on([chip], 0)
        order = looked_up([arrival_order(chip_, chips) for chip_ in range(chips)], chip)
        groups, taken = [], 0
        while taken < len(order):
            count = FIRST_GROUPS[len(groups)] if len(groups) < len(FIRST_GROUPS) else 2
            groups.append((order[taken:taken + count], 1 + taken))
            taken += count
        middle = len(every) // 2
        before = None
        for turn, (group, place) in enumerate(groups):
            await_templates(group)
            if turn == max(len(groups) - 3, 0):
                halo_copy(0).wait_recv()
                prepare_edge()
            for i, slot in enumerate(group):
                stagger(slot, place + i)
            if before is not None:
                correlate(*before[1:], every[middle:])
                keep(*before[:2])
            best = unseen(group)
            last = turn == len(groups) - 1
            correlate(best, place, every if last else every[:middle])
            before = (group, best, place)
        keep(*before[:2])
    else:
        halo_copy(0).wait_recv()
        prepare_edge()
        lax.fori_loop(0, slots, lambda slot, _: (work_on([slot], 0), 0)[1], 0)

    block = jnp.concatenate(
        [hankel[:, pl.ds(c * LANES, extra * LANES)] for c in range(extra)], axis=0)
    e_totals, e_scales = edge_stats[0], edge_stats[1]
    templates = gathered[...].astype(jnp.float32).reshape(-1, width).astype(jnp.bfloat16)
    products = jnp.dot(templates, block, preferred_element_type=jnp.float32)
    means = mean_ref[...]
    edge = jnp.full(means.shape, -jnp.inf, jnp.float32)
    for tile in range(extra):
        score = ((products[:, tile * LANES:(tile + 1) * LANES] - e_totals[tile:tile + 1] * means)
                 * e_scales[tile:tile + 1])
        last = (lanes_held - extra + tile) * LANES + lane
        usable = inner | (last <= lanes_held * LANES - width)
        edge = jnp.maximum(edge, jnp.where(usable, score, -jnp.inf))
    best = best_ref[...].reshape(slots, 2, SUBLANES, LANES)
    edge = edge.reshape(slots, SUBLANES, LANES)
    best = jnp.concatenate(
        [part for slot in range(slots)
         for part in (best[slot, 0], jnp.maximum(best[slot, 1], edge[slot]))], axis=0)
    best = best / norm_ref[...]
    rho = jnp.max(best.T, axis=0, keepdims=True)
    distance = jnp.sqrt(jnp.maximum(2.0 - 2.0 * rho, 0.0))
    mine[...] = distance
    minima[me] = distance

    def out_copy(step):
        return pltpu.make_async_remote_copy(
            src_ref=mine, dst_ref=minima.at[me],
            send_sem=out_sems.at[0], recv_sem=out_sems.at[1],
            device_id=(grp, peer(step)), device_id_type=MESH)

    each(n - 1, lambda step: out_copy(step).start())
    others = minima.at[pl.ds(0, n - 1)]
    arrivals = pltpu.make_async_remote_copy(
        src_ref=others, dst_ref=others, send_sem=out_sems.at[0], recv_sem=out_sems.at[1],
        device_id=(grp, sibling), device_id_type=MESH)
    pair_copy.wait_send()
    if gathers and chips > 1:
        template_wait(0, chips - 1, 0).wait_send()
    arrivals.wait_send()

    @pl.when(sends_halo)
    def _():
        for target in range(2):
            halo_copy(target).wait_send()

    arrivals.wait_recv()

    queries = both_ref.shape[1]
    place = lax.broadcasted_iota(jnp.int32, (1, queries), 1)
    even = lax.rem(place // SUBLANES, 2) == 0

    def earlier(row):
        return pltpu.roll(row, queries - SUBLANES, 1)

    def later(row):
        return pltpu.roll(row, SUBLANES, 1)

    first, second = minima[chip * 2], minima[chip * 2 + 1]
    profile = jnp.where(
        core == 0, jnp.where(even, first, later(second)), jnp.where(even, earlier(first), second))
    found = jnp.min(minima[...].reshape(chips, 2, 1, queries), axis=0)
    overall = jnp.where(
        even, jnp.minimum(found[0], earlier(found[0])), jnp.minimum(found[1], later(found[1])))
    both_ref[...] = jnp.concatenate([profile, overall], axis=0)


def per_device(n, strain, templates):
    held, width = templates.shape
    queries = n * held
    slots = queries // PACKED
    gathers = held == SUBLANES
    if not gathers:
        templates = lax.all_gather(templates, "seg", axis=0, tiled=True)
        templates = jnp.swapaxes(templates.reshape(slots, 2, SUBLANES, width), 0, 1)
    rows = strain.shape[0] // LANES
    extra = width // LANES
    dma = pltpu.SemaphoreType.DMA
    f32, bf16 = jnp.float32, jnp.bfloat16
    both = pl.pallas_call(
        functools.partial(kernel, n, width, gathers),
        out_shape=pltpu.VMEM((2, queries), f32),
        in_specs=[pl.BlockSpec(memory_space=pl.ANY)] * 2,
        out_specs=pl.BlockSpec(memory_space=pltpu.VMEM),
        scratch_shapes=[
            pltpu.VMEM((2, rows, LANES), bf16),
            pltpu.VMEM((SUBLANES, width), bf16),
            pltpu.VMEM((PACKED, LANES), bf16),
            pltpu.VMEM((slots, SUBLANES, width), bf16),
            pltpu.VMEM((width + LANES, 2 * rows), bf16),
            pltpu.VMEM((LANES // PACKED * CENTRES, 2 * rows), bf16),
            pltpu.VMEM((LANES, 2 * rows), f32),
            pltpu.VMEM(((slots if gathers else 1) * SUBLANES * PACKED, width + LANES), bf16),
            pltpu.VMEM((queries, LANES), f32),
            pltpu.VMEM((queries // 2, LANES), f32),
            pltpu.VMEM((queries, LANES), f32),
            pltpu.VMEM((2 * extra, PACKED, LANES), f32),
            pltpu.VMEM((LANES, 2 * extra * LANES), bf16),
            pltpu.VMEM((2, 2, PACKED, LANES), f32),
            pltpu.VMEM((2, extra, LANES), f32),
            pltpu.VMEM((n, 1, queries), f32),
            pltpu.VMEM((1, queries), f32),
            dma((2,)), dma((2,)), dma((3,)), dma, dma((slots,)), dma((2,)),
        ],
        compiler_params=pltpu.CompilerParams(collective_id=0, has_side_effects=True),
    )(strain.reshape(rows, LANES), templates)
    return (both[:1], both[1])


def solution(mesh):
    in_specs = (P(("grp", "seg")), P("seg", None))
    out_specs = (P(("grp", "seg"), None), P("grp"))
    return jax.shard_map(
        functools.partial(per_device, mesh.shape["seg"]),
        mesh=mesh, in_specs=in_specs, out_specs=out_specs, check_vma=False,
    )
```

```python
import functools

import jax
import jax.numpy as jnp
from jax import lax
from jax.experimental import pallas as pl
from jax.experimental.pallas import tpu as pltpu
from jax.sharding import PartitionSpec as P

EPSILON = 1e-05
LANES = 128
SUBLANES = 8
PACKED = 16
CENTRES = 112
FIRST_GROUPS = (2, 1)
TERMS = ((0, 0), (0, 1), (1, 0), (0, 2), (1, 1), (2, 0))
MESH = pl.DeviceIdType.MESH


def each(count, body):
    if count <= 16:
        for step in range(count):
            body(step)
    else:
        lax.fori_loop(0, count, lambda step, _: (body(step), 0)[1], 0)


def hops(me, other):
    return abs(other // 2 - me // 2) + abs(other % 2 - me % 2)


def send_order(me, chips):
    others = [other for other in range(chips) if other != me]
    if me // 2 == (chips - 1) // 2:
        return sorted(others, key=lambda other: (other // 2 != me // 2, other // 2, hops(me, other)))
    return sorted(others, key=lambda other: (-(other // 2), -hops(me, other)))


def arrival_order(me, chips):
    def expected(other):
        entry = (chips - 2 - other // 2 * 2) * 5
        return entry + 2 * send_order(other, chips).index(me) + 11 * hops(me, other)

    return sorted((other for other in range(chips) if other != me), key=expected)


def looked_up(table, chip):
    return [sum(jnp.where(chip == me, row[step], 0) for me, row in enumerate(table)) for step in range(len(table[0]))]


def bf16_parts(square):
    high = square.astype(jnp.bfloat16)
    return high, (square - high.astype(jnp.float32)).astype(jnp.bfloat16)


def bf16_split(value):
    parts = []
    for _ in range(3):
        parts.append(value.astype(jnp.bfloat16))
        value = value - parts[-1].astype(jnp.float32)
    return parts


def deviation(totals, squared, width):
    win_mean = totals / width
    return jnp.sqrt(jnp.maximum(squared / width - win_mean * win_mean, 0.0) + EPSILON)


def edge_sums(parts, work, rows, extra):
    source = lax.broadcasted_iota(jnp.int32, (LANES, 2 * LANES), 0)
    place = lax.broadcasted_iota(jnp.int32, (LANES, 2 * LANES), 1)
    from_place = (place < LANES) & (source >= place)
    to_place = (place >= LANES) & (source < place - LANES)
    ones = jnp.where(from_place | to_place, 1.0, 0.0).astype(jnp.bfloat16)
    both = sum(jnp.dot(part, ones, preferred_element_type=jnp.float32) for part in parts)
    first, last = both[:, :LANES], both[:, LANES:]
    work[0] = first + last
    work[1] = last
    total = first[:rows]
    for row in range(1, extra):
        total = total + work[0, pl.ds(row, rows), :]
    return total + work[1, pl.ds(extra, rows), :]


def kernel(n, width, gathers, strain_any, templates_any, both_ref,
           pair, templates_ref, halo, gathered, columns, centres, scales, leads,
           best_ref, mean_ref, norm_ref, near, hankel, work, edge_stats, minima, mine,
           local, pair_sems, halo_sems, t_send, t_recv, out_sems):
    me = lax.axis_index("seg")
    grp = lax.axis_index("grp")
    chip, core = me // 2, me % 2
    chips = n // 2
    sibling = chip * 2 + 1 - core
    rows = pair.shape[1]
    lanes_held = 2 * rows
    extra = width // LANES
    depth = width + LANES
    slots = gathered.shape[0]

    def peer(step):
        down = n - 1 - step
        down = jnp.where(down <= me, down - 1, down)
        up = jnp.where(step >= me, step + 1, step)
        return jnp.where(me * 2 < n, down, up)

    fetches = [
        pltpu.make_async_copy(strain_any, pair.at[core], local.at[0]),
        pltpu.make_async_copy(templates_any, templates_ref, local.at[1]) if gathers
        else pltpu.make_async_copy(templates_any.at[core], gathered, local.at[1]),
    ]
    for fetch in fetches:
        fetch.start()
    barrier = pltpu.get_barrier_semaphore()
    each(n - 1, lambda step: pl.semaphore_signal(
        barrier, inc=1, device_id=(grp, peer(step)), device_id_type=MESH))

    for fetch in fetches:
        fetch.wait()

    pl.semaphore_wait(barrier, n - 1)

    pair_copy = pltpu.make_async_remote_copy(
        src_ref=pair.at[core], dst_ref=pair.at[core],
        send_sem=pair_sems.at[0], recv_sem=pair_sems.at[1],
        device_id=(grp, sibling), device_id_type=MESH)

    def halo_copy(target):
        return pltpu.make_async_remote_copy(
            src_ref=pair.at[0, pl.ds(0, PACKED)], dst_ref=halo,
            send_sem=halo_sems.at[target], recv_sem=halo_sems.at[2],
            device_id=(grp, jnp.maximum(chip - 1, 0) * 2 + target), device_id_type=MESH)

    def template_copy(target):
        return pltpu.make_async_remote_copy(
            src_ref=templates_ref, dst_ref=gathered.at[chip],
            send_sem=t_send, recv_sem=t_recv.at[chip],
            device_id=(grp, target * 2 + core), device_id_type=MESH)

    def template_wait(start, count, sem):
        part = gathered.at[pl.ds(start, count)]
        return pltpu.make_async_remote_copy(
            src_ref=part, dst_ref=part, send_sem=t_send, recv_sem=t_recv.at[sem],
            device_id=(grp, sibling), device_id_type=MESH)

    targets = looked_up([send_order(chip_, chips) for chip_ in range(chips)], chip) if gathers else []
    inner = chip < chips - 1
    sends_halo = (chip > 0) & (core == 0)
    no_halo = pltpu.make_async_copy(pair.at[core, pl.ds(0, PACKED)], halo, halo_sems.at[2])
    pair_copy.start()
    for target in targets[:4]:
        template_copy(target).start()

    @pl.when(sends_halo)
    def _():
        for target in range(2):
            halo_copy(target).start()

    @pl.when(jnp.logical_not(inner))
    def _():
        no_halo.start()

    for target in targets[4:]:
        template_copy(target).start()
    if gathers:
        gathered[chip] = templates_ref[...]

    lane = lax.broadcasted_iota(jnp.int32, (1, LANES), 1)

    def rows_of(slot, count):
        return pl.ds(pl.multiple_of(slot * count, count), count)

    def stagger(slot, place):
        floats = gathered[slot].astype(jnp.float32)
        t_mean = jnp.mean(floats, axis=1, keepdims=True)
        t_dev = jnp.sqrt(jnp.mean((floats - t_mean) ** 2, axis=1, keepdims=True) + EPSILON)
        means = bf16_split(t_mean)
        beyond = jnp.zeros((SUBLANES, LANES), jnp.float32)
        for j, (_, part) in enumerate(TERMS):
            beyond = jnp.where(lane == (j + 1) * PACKED, -means[part].astype(jnp.float32), beyond)
        padded = jnp.concatenate([floats, beyond], axis=1)
        padded = jnp.concatenate([padded, pltpu.roll(padded, SUBLANES, 1)], axis=0).astype(jnp.bfloat16)
        for shift in range(SUBLANES):
            leads[pl.ds((place * SUBLANES + shift) * PACKED, PACKED), :] = (
                padded if shift == 0 else pltpu.roll(padded, shift, 1))
        mean_ref[rows_of(slot, SUBLANES), :] = jnp.broadcast_to(t_mean, (SUBLANES, LANES))
        norm_ref[rows_of(slot, PACKED), :] = jnp.broadcast_to(
            jnp.concatenate([width * t_dev] * 2, axis=0), (PACKED, LANES))

    def unseen(group):
        return [[jnp.full((SUBLANES, lanes_held), -jnp.inf, jnp.float32) for _ in range(2)] for _ in group]

    def correlate(best, place, firsts):
        lead = leads[pl.ds(place * SUBLANES * PACKED, len(best) * SUBLANES * PACKED), :]
        for first in firsts:
            samples = jnp.concatenate(
                [columns[pl.ds(first, width + PACKED), :],
                 centres[pl.ds(first * CENTRES // PACKED, CENTRES), :]], axis=0)
            products = jnp.dot(lead, samples, preferred_element_type=jnp.float32)
            for shift in range(PACKED):
                scale = scales[pl.ds(first + shift, 1), :]
                within = shift % SUBLANES * PACKED + shift // SUBLANES * SUBLANES
                for i, found in enumerate(best):
                    top = i * SUBLANES * PACKED + within
                    found[shift % 2] = jnp.maximum(
                        found[shift % 2], products[top:top + SUBLANES] * scale)

    def keep(group, best):
        for slot, found in zip(group, best):
            found = jnp.maximum(found[0], found[1])
            ahead = jnp.where(lane < rows - extra, found[:, rows:], -jnp.inf)
            best_ref[rows_of(slot, PACKED), :] = jnp.concatenate([found[:, :rows], ahead], axis=0)

    every = range(0, LANES, PACKED)

    def work_on(group, place):
        for i, slot in enumerate(group):
            stagger(slot, place + i)
        best = unseen(group)
        correlate(best, place, every)
        keep(group, best)

    def await_templates(group):
        for slot in group:
            template_wait(slot, 1, slot).wait_recv()

    pair_copy.wait_recv()

    strain = jnp.concatenate([pair[0].astype(jnp.float32), pair[1].astype(jnp.float32)], axis=0)
    turned = strain.T.astype(jnp.bfloat16)
    for step in range(extra + 1):
        columns[pl.ds(step * LANES, LANES), :] = (
            turned if step == 0 else pltpu.roll(turned, lanes_held - step, 1))

    window = lax.broadcasted_iota(jnp.int32, (LANES, depth), 0)
    sample = lax.broadcasted_iota(jnp.int32, (LANES, depth), 1)
    band = jnp.where((sample >= window) & (sample < window + width), 1.0, 0.0).astype(jnp.bfloat16)
    held = columns[...]
    wide = held.astype(jnp.float32)
    high, low = bf16_parts(wide * wide)
    totals = jnp.dot(band, held, preferred_element_type=jnp.float32)
    squared = (jnp.dot(band, high, preferred_element_type=jnp.float32)
               + jnp.dot(band, low, preferred_element_type=jnp.float32))
    parts = bf16_split(totals)
    for first in range(0, LANES, PACKED):
        start = first * CENTRES // PACKED
        for j, (part, _) in enumerate(TERMS):
            centres[pl.ds(start + j * PACKED, PACKED), :] = parts[part][first:first + PACKED]
        centres[pl.ds(start + CENTRES - PACKED, PACKED), :] = jnp.zeros((PACKED, lanes_held), jnp.bfloat16)
    scales[...] = 1.0 / deviation(totals, squared, width)

    def prepare_edge():
        following = jnp.where(inner, halo[...].astype(jnp.float32)[:extra], 0.0)
        samples = jnp.concatenate(
            [pair[1].astype(jnp.float32)[rows - extra:], following,
             jnp.zeros((PACKED - 2 * extra, LANES), jnp.float32)], axis=0)
        tiles = 2 * extra
        lanes = lax.broadcasted_iota(jnp.int32, (tiles, LANES), 1)
        near[:, 0, :] = samples[:tiles]
        for shift in range(1, PACKED):
            near[:, shift, :] = pltpu.roll(
                jnp.where(lanes >= shift, samples[:tiles], samples[1:tiles + 1]), LANES - shift, 1)
        span = tiles * LANES
        shifted = near[...].astype(jnp.bfloat16)
        base = jnp.concatenate([shifted[i] for i in range(tiles)], axis=1)
        for group in range(LANES // PACKED):
            turned = base if group == 0 else pltpu.roll(base, span - group * PACKED, 1)
            hankel[pl.ds(group * PACKED, PACKED), :] = turned
        e_totals = edge_sums([samples.astype(jnp.bfloat16)], work.at[0], extra, extra)
        e_squared = edge_sums(list(bf16_parts(samples * samples)), work.at[1], extra, extra)
        e_scales = 1.0 / deviation(e_totals, e_squared, width)
        edge_stats[0] = e_totals
        edge_stats[1] = e_scales

    if gathers:
        work_on([chip], 0)
        order = looked_up([arrival_order(chip_, chips) for chip_ in range(chips)], chip)
        groups, taken = [], 0
        while taken < len(order):
            count = FIRST_GROUPS[len(groups)] if len(groups) < len(FIRST_GROUPS) else 2
            groups.append((order[taken:taken + count], 1 + taken))
            taken += count
        middle = len(every) // 2
        before = None
        for turn, (group, place) in enumerate(groups):
            await_templates(group)
            if turn == max(len(groups) - 3, 0):
                halo_copy(0).wait_recv()
                prepare_edge()
            for i, slot in enumerate(group):
                stagger(slot, place + i)
            if before is not None:
                correlate(*before[1:], every[middle:])
                keep(*before[:2])
            best = unseen(group)
            last = turn == len(groups) - 1
            correlate(best, place, every if last else every[:middle])
            before = (group, best, place)
        keep(*before[:2])
    else:
        halo_copy(0).wait_recv()
        prepare_edge()
        lax.fori_loop(0, slots, lambda slot, _: (work_on([slot], 0), 0)[1], 0)

    block = jnp.concatenate(
        [hankel[:, pl.ds(c * LANES, extra * LANES)] for c in range(extra)], axis=0)
    e_totals, e_scales = edge_stats[0], edge_stats[1]
    templates = gathered[...].astype(jnp.float32).reshape(-1, width).astype(jnp.bfloat16)
    products = jnp.dot(templates, block, preferred_element_type=jnp.float32)
    means = mean_ref[...]
    edge = jnp.full(means.shape, -jnp.inf, jnp.float32)
    for tile in range(extra):
        score = ((products[:, tile * LANES:(tile + 1) * LANES] - e_totals[tile:tile + 1] * means)
                 * e_scales[tile:tile + 1])
        last = (lanes_held - extra + tile) * LANES + lane
        usable = inner | (last <= lanes_held * LANES - width)
        edge = jnp.maximum(edge, jnp.where(usable, score, -jnp.inf))
    best = best_ref[...].reshape(slots, 2, SUBLANES, LANES)
    edge = edge.reshape(slots, SUBLANES, LANES)
    best = jnp.concatenate(
        [part for slot in range(slots)
         for part in (best[slot, 0], jnp.maximum(best[slot, 1], edge[slot]))], axis=0)
    best = best / norm_ref[...]
    rho = jnp.max(best.T, axis=0, keepdims=True)
    distance = jnp.sqrt(jnp.maximum(2.0 - 2.0 * rho, 0.0))
    mine[...] = distance
    minima[me] = distance

    def out_copy(step):
        return pltpu.make_async_remote_copy(
            src_ref=mine, dst_ref=minima.at[me],
            send_sem=out_sems.at[0], recv_sem=out_sems.at[1],
            device_id=(grp, peer(step)), device_id_type=MESH)

    each(n - 1, lambda step: out_copy(step).start())
    others = minima.at[pl.ds(0, n - 1)]
    arrivals = pltpu.make_async_remote_copy(
        src_ref=others, dst_ref=others, send_sem=out_sems.at[0], recv_sem=out_sems.at[1],
        device_id=(grp, sibling), device_id_type=MESH)
    pair_copy.wait_send()
    if gathers and chips > 1:
        template_wait(0, chips - 1, 0).wait_send()
    arrivals.wait_send()

    @pl.when(sends_halo)
    def _():
        for target in range(2):
            halo_copy(target).wait_send()

    arrivals.wait_recv()

    queries = both_ref.shape[1]
    place = lax.broadcasted_iota(jnp.int32, (1, queries), 1)
    even = lax.rem(place // SUBLANES, 2) == 0

    def earlier(row):
        return pltpu.roll(row, queries - SUBLANES, 1)

    def later(row):
        return pltpu.roll(row, SUBLANES, 1)

    first, second = minima[chip * 2], minima[chip * 2 + 1]
    profile = jnp.where(
        core == 0, jnp.where(even, first, later(second)), jnp.where(even, earlier(first), second))
    found = jnp.min(minima[...].reshape(chips, 2, 1, queries), axis=0)
    overall = jnp.where(
        even, jnp.minimum(found[0], earlier(found[0])), jnp.minimum(found[1], later(found[1])))
    both_ref[...] = jnp.concatenate([profile, overall], axis=0)


def per_device(n, strain, templates):
    held, width = templates.shape
    queries = n * held
    slots = queries // PACKED
    gathers = held == SUBLANES
    if not gathers:
        templates = lax.all_gather(templates, "seg", axis=0, tiled=True)
        templates = jnp.swapaxes(templates.reshape(slots, 2, SUBLANES, width), 0, 1)
    rows = strain.shape[0] // LANES
    extra = width // LANES
    dma = pltpu.SemaphoreType.DMA
    f32, bf16 = jnp.float32, jnp.bfloat16
    both = pl.pallas_call(
        functools.partial(kernel, n, width, gathers),
        out_shape=pltpu.VMEM((2, queries), f32),
        in_specs=[pl.BlockSpec(memory_space=pl.ANY)] * 2,
        out_specs=pl.BlockSpec(memory_space=pltpu.VMEM),
        scratch_shapes=[
            pltpu.VMEM((2, rows, LANES), bf16),
            pltpu.VMEM((SUBLANES, width), bf16),
            pltpu.VMEM((PACKED, LANES), bf16),
            pltpu.VMEM((slots, SUBLANES, width), bf16),
            pltpu.VMEM((width + LANES, 2 * rows), bf16),
            pltpu.VMEM((LANES // PACKED * CENTRES, 2 * rows), bf16),
            pltpu.VMEM((LANES, 2 * rows), f32),
            pltpu.VMEM(((slots if gathers else 1) * SUBLANES * PACKED, width + LANES), bf16),
            pltpu.VMEM((queries, LANES), f32),
            pltpu.VMEM((queries // 2, LANES), f32),
            pltpu.VMEM((queries, LANES), f32),
            pltpu.VMEM((2 * extra, PACKED, LANES), f32),
            pltpu.VMEM((LANES, 2 * extra * LANES), bf16),
            pltpu.VMEM((2, 2, PACKED, LANES), f32),
            pltpu.VMEM((2, extra, LANES), f32),
            pltpu.VMEM((n, 1, queries), f32),
            pltpu.VMEM((1, queries), f32),
            dma((2,)), dma((2,)), dma((3,)), dma, dma((slots,)), dma((2,)),
        ],
        compiler_params=pltpu.CompilerParams(collective_id=0, has_side_effects=True),
    )(strain.reshape(rows, LANES), templates)
    return (both[:1], both[1])


def solution(mesh):
    in_specs = (P(("grp", "seg")), P("seg", None))
    out_specs = (P(("grp", "seg"), None), P("grp"))
    return jax.shard_map(
        functools.partial(per_device, mesh.shape["seg"]),
        mesh=mesh, in_specs=in_specs, out_specs=out_specs, check_vma=False,
    )
```
